32 devices in a mesh: layer: 4 (over y, x), expert: 4 (over z), dp: 2 (over core).
Axes of the slice: x: 2, y: 2, z: 4, core: 2. Of those that a mesh axis runs over, the one named last changes fastest.
Arguments:
- tokens: bfloat16 [2048, 2304], P(('expert', 'dp')), may hold values from -6 to 6
- expert_ids: int32 [2048], P(('expert', 'dp')), may hold values from 0 to 3, as said below
- slot_ids: int32 [2048], P(('expert', 'dp')), may hold values from 0 to 127, as said below
- live_mask: int32 [2048], P(('expert', 'dp')), may hold values from 0 to 1
- w_enc: bfloat16 [4, 2304, 2048], P('expert', None, 'layer'), may hold values from -0.125 to 0.125
- b_enc: float32 [4, 2048], P('expert', 'layer'), may hold values from -3 to 3
- w_dec: bfloat16 [2, 4, 2048, 2304], P(None, 'expert', 'layer'), may hold values from -0.125 to 0.125
- b_dec: float32 [2, 2304], P(None, 'layer'), may hold values from -3 to 3
- targets: bfloat16 [2, 2048, 2304], P(None, ('expert', 'dp'), 'layer'), may hold values from -6 to 6
Outputs:
- recon: bfloat16 [2, 2048, 2304], P(None, ('expert', 'dp'), 'layer')
- grad_w_enc: bfloat16 [4, 2304, 2048], P('expert', 'dp', 'layer')
- grad_b_enc: float32 [4, 2048], P('expert', ('layer', 'dp'))
- grad_w_dec: bfloat16 [2, 4, 2048, 2304], P(None, 'expert', 'layer', 'dp')
- grad_b_dec: float32 [2, 2304], P(None, 'layer')
The draws below stay inside these ranges and needn't reach their ends.
Inputs may be any that keep to these rules, and one draw needn't show every extreme that they name: `expert_ids`: the 256 tokens of one block name any expert at most 128 times; in every draw one expert is named exactly 128 times by every block. `slot_ids`: tokens of one block that name the same expert have distinct slots.
All inputs are finite; a program needn't handle non-finite values.
Results may differ from the reference program's by a relative error of at most 0.01.
Values may be sent and summed in bfloat16 or wider, within the bound.
A program may use at most 128 MiB of HBM per device.

```python
import math
import jax
import jax.numpy as jnp
from jax import lax

D = 2304
LAT = 2048
TGT = 2
TOK_DEV = 256
EXPERTS = 4
BLOCKS = 8
TOKENS = 2048
CAP = 128
N_LAYER = 4


def route_cells(key):
    base = jax.random.fold_in(key, 7301)
    busiest = jax.random.randint(jax.random.fold_in(base, 1), (), 0, EXPERTS)
    block_keys = jax.random.split(jax.random.fold_in(base, 2), BLOCKS)
    total_cells = EXPERTS * CAP

    def one_block(block_key):
        key_order, key_second, key_tokens = jax.random.split(block_key, 3)
        cell_ids = jnp.arange(total_cells, dtype=jnp.int32)
        owner_id = cell_ids // CAP
        second = jax.random.randint(key_second, (), 0, EXPERTS)
        tier_rank = jnp.where(owner_id == busiest, 0, jnp.where(owner_id == second, 1, 2)).astype(jnp.int32)
        cell_rank = jnp.argsort(jax.random.permutation(key_order, total_cells)).astype(jnp.int32)
        cell_order = jnp.argsort(tier_rank * total_cells + cell_rank).astype(jnp.int32)
        chosen = cell_order[:TOK_DEV]
        shuffled = chosen[jax.random.permutation(key_tokens, TOK_DEV)]
        return (shuffled // CAP, shuffled % CAP)
    experts_all, slots_all = jax.vmap(one_block)(block_keys)
    return (experts_all.reshape(TOKENS).astype(jnp.int32), slots_all.reshape(TOKENS).astype(jnp.int32))


def draw_expert_ids(key, part):
    return route_cells(key)[0]


def draw_slot_ids(key, part):
    return route_cells(key)[1]


def draw_live_mask(key, part):
    lengths = jax.random.randint(jax.random.fold_in(key, 9157), (BLOCKS,), TOK_DEV // 4, TOK_DEV + 1)
    positions = jnp.arange(TOK_DEV, dtype=jnp.int32)
    return (positions[None, :] < lengths[:, None]).astype(jnp.int32).reshape(TOKENS)


def level_of(rng, dims, cuts, low, high):
    factor_of = 1.0
    for position, parts in cuts:
        heights = jax.random.uniform(jax.random.fold_in(jax.random.fold_in(rng, 6), position), (parts,), jnp.float32, low / len(cuts), high / len(cuts))
        factor_of = factor_of * jnp.repeat(jnp.exp(heights), dims[position] // parts).reshape((-1,) + (1,) * (len(dims) - 1 - position))
    return factor_of


def centred(rng, extent, width, limit, cuts=(), kind=jnp.bfloat16):
    array = width * jax.random.normal(rng, extent, jnp.float32)
    if cuts:
        array = array * level_of(rng, extent, cuts, -0.22, 0.18)
    return jnp.clip(array, -limit, limit).astype(kind)


def setup_inputs(seed: int = 0) -> dict:
    key_list = jax.random.split(jax.random.key(seed), 10)
    tokens = centred(key_list[0], (TOKENS, D), 1.0, 6.0, ((0, 8),))
    expert_ids = draw_expert_ids(jax.random.fold_in(key_list[9], 71), 0)
    slot_ids = draw_slot_ids(jax.random.fold_in(key_list[9], 71), 0)
    live_mask = draw_live_mask(jax.random.fold_in(key_list[9], 71), 0)
    w_enc = centred(key_list[4], (EXPERTS, D, LAT), D ** -0.5, 0.125, ((0, 4), (2, 4)))
    b_enc = centred(key_list[5], (EXPERTS, LAT), 0.5, 3.0, ((0, 4), (1, 4)), jnp.float32)
    w_dec = centred(key_list[6], (TGT, EXPERTS, LAT, D), LAT ** -0.5, 0.125, ((1, 4), (2, 4)))
    b_dec = centred(key_list[7], (TGT, D), 0.5, 3.0, ((1, 4),), jnp.float32)
    targets = centred(key_list[8], (TGT, TOKENS, D), 1.0, 6.0, ((1, 8), (2, 4)))
    return dict(tokens=tokens, expert_ids=expert_ids, slot_ids=slot_ids, live_mask=live_mask, w_enc=w_enc, b_enc=b_enc, w_dec=w_dec, b_dec=b_dec, targets=targets)


def reference(tokens, expert_ids, slot_ids, live_mask, w_enc, b_enc, w_dec, b_dec, targets):
    coef = 2.0 / math.sqrt(TOK_DEV)
    rows_expert = BLOCKS * CAP
    quarter = LAT // N_LAYER
    token_ids = jnp.arange(TOKENS, dtype=jnp.int32)
    row_ids = (token_ids // TOK_DEV * CAP + slot_ids).astype(jnp.int32)
    row_table = jnp.full((EXPERTS, rows_expert), TOKENS, jnp.int32).at[expert_ids, row_ids].set(token_ids)
    tokens_pad = jnp.concatenate([tokens, jnp.zeros((1, D), tokens.dtype)], axis=0)
    targets_pad = jnp.concatenate([targets, jnp.zeros((TGT, 1, D), targets.dtype)], axis=1)
    live_pad = jnp.concatenate([live_mask, jnp.zeros((1,), jnp.int32)]).astype(jnp.float32)

    def one_expert(carry_state, expert):
        recon_out, bias_total = carry_state
        expert_rows = row_table[expert]
        inputs = tokens_pad[expert_rows]
        pre_act = jnp.dot(inputs, w_enc[expert], preferred_element_type=jnp.float32) + b_enc[expert][None, :]
        active = jnp.maximum(pre_act, 0.0)
        latents = (active * active).astype(jnp.bfloat16)
        rebuilt = []
        for target in range(TGT):
            summed = jnp.zeros((rows_expert, D), jnp.float32)
            for quarter_id in range(N_LAYER):
                first = quarter_id * quarter
                partial_value = jnp.dot(latents[:, first:first + quarter], w_dec[target, expert, first:first + quarter], preferred_element_type=jnp.float32).astype(jnp.bfloat16)
                summed = summed + lax.optimization_barrier(partial_value).astype(jnp.float32)
            rebuilt.append(summed.astype(jnp.bfloat16))
        recon_sum = jnp.stack(rebuilt)
        recon_full = lax.optimization_barrier(recon_sum).astype(jnp.float32) + b_dec[:, None, :]
        recon_rows = recon_full.astype(jnp.bfloat16)
        wanted = targets_pad[:, expert_rows].astype(jnp.float32)
        live_rows = live_pad[expert_rows]
        error_grad = (coef * live_rows[None, :, None] * (recon_full - wanted)).astype(jnp.bfloat16)
        error_wide = lax.optimization_barrier(error_grad).astype(jnp.float32)
        bias_total = bias_total + lax.optimization_barrier(jnp.sum(error_wide, axis=1))
        latent_wide = latents.astype(jnp.float32)
        grad_dec = jnp.einsum('rl,trd->tld', latent_wide, error_wide)
        grad_latent = jnp.einsum('trd,tld->rl', error_wide, w_dec[:, expert].astype(jnp.float32))
        grad_pre = (grad_latent * (2.0 * active)).astype(jnp.bfloat16)
        grad_wide = lax.optimization_barrier(grad_pre).astype(jnp.float32)
        grad_enc = jnp.einsum('rd,rl->dl', inputs.astype(jnp.float32), grad_wide)
        grad_bias = lax.optimization_barrier(jnp.sum(grad_wide, axis=0))
        recon_out = recon_out.at[:, expert_rows].set(recon_rows)
        return ((recon_out, bias_total), (grad_enc.astype(jnp.bfloat16), grad_bias, grad_dec.astype(jnp.bfloat16)))
    initial = (jnp.zeros((TGT, TOKENS + 1, D), jnp.bfloat16), jnp.zeros((TGT, D), jnp.float32))
    (recon_out, bias_total), (grad_w_enc, grad_b_enc, grad_stack) = lax.scan(one_expert, initial, jnp.arange(EXPERTS, dtype=jnp.int32))
    grad_w_dec = jnp.swapaxes(grad_stack, 0, 1)
    return (recon_out[:, :TOKENS], grad_w_enc, grad_b_enc, grad_w_dec, bias_total)
```

```python
import math

import jax
import jax.numpy as jnp
from jax import lax
from jax.sharding import PartitionSpec as P


def local(tokens, expert_ids, slot_ids, live_mask, w_enc, b_enc, w_dec, b_dec, targets):
    f32, bf16 = jnp.float32, jnp.bfloat16
    n_expert = lax.axis_size("expert")
    n_layer = lax.axis_size("layer")
    n_dp = lax.axis_size("dp")
    tok_rows, model_width = tokens.shape
    capacity = 2 * tok_rows // n_expert
    total_cells = n_expert * capacity
    cell_index = expert_ids * capacity + slot_ids
    quarter = model_width // n_layer
    targets_count = w_dec.shape[0]
    enc_weight = w_enc[0]
    place = (
        lax.broadcasted_iota(jnp.int32, (total_cells, tok_rows), 0) == cell_index[None, :]
    ).astype(bf16)

    cells = lax.dot_general(
        tokens, place, (((0,), (1,)), ((), ())), preferred_element_type=f32
    ).astype(bf16)
    own = lax.dynamic_slice_in_dim(cells, lax.axis_index("layer") * quarter, quarter, 0)
    arrived_part = lax.all_to_all(own, "expert", split_axis=1, concat_axis=1, tiled=True)
    arrived = lax.all_gather(arrived_part, "layer", axis=0, tiled=True)
    pre_act = jnp.einsum("dr,dl->rl", arrived, enc_weight, preferred_element_type=f32)
    pre_act = pre_act + b_enc[0][None, :]
    active = jnp.maximum(pre_act, 0.0)
    latents = (active * active).astype(bf16)

    coef = 2.0 / math.sqrt(tok_rows)
    live_wide = live_mask.astype(f32)
    partials = [
        jnp.einsum("ld,rl->dr", w_dec[t, 0], latents, preferred_element_type=f32).astype(bf16)
        for t in range(targets_count)
    ]
    summed = [
        lax.psum_scatter(p, "layer", scatter_dimension=0, tiled=True) for p in partials
    ]
    recons, errors, segments = [], [], []
    for t in range(targets_count):
        returned = lax.all_to_all(summed[t], "expert", split_axis=1, concat_axis=1, tiled=True)
        recon_sum = jnp.einsum("dr,ri->di", returned, place, preferred_element_type=f32)
        recon_full = recon_sum + b_dec[t][:, None]
        recons.append(recon_full.astype(bf16).T)
        error = (
            coef * live_wide[None, :] * (recon_full - targets[t].T.astype(f32))
        ).astype(bf16)
        errors.append(jnp.sum(error.astype(f32), axis=1))
        outgoing = jnp.einsum(
            "di,ri->dr", error, place, preferred_element_type=f32
        ).astype(bf16)
        part = lax.all_to_all(outgoing, "expert", split_axis=1, concat_axis=1, tiled=True)
        segments.append(lax.all_gather(part, "layer", axis=0, tiled=True))
    recon = jnp.stack(recons)
    error_sums = lax.all_gather(jnp.stack(errors), ("expert", "dp"), axis=0)
    grad_b_dec = jnp.sum(error_sums, axis=0)

    grad_lat = sum(
        jnp.einsum("dr,ld->rl", segments[t], w_dec[t, 0], preferred_element_type=f32)
        for t in range(targets_count)
    )
    dec_parts = [
        lax.psum_scatter(
            jnp.einsum(
                "rl,hdr->hld",
                latents,
                segments[t].reshape(n_dp, model_width // n_dp, total_cells),
                preferred_element_type=f32,
            ).astype(bf16),
            "dp",
            scatter_dimension=0,
            tiled=True,
        )
        for t in range(targets_count)
    ]
    grad_pre = (grad_lat * (2.0 * active)).astype(bf16)
    grad_enc = jnp.einsum("dr,rl->dl", arrived, grad_pre, preferred_element_type=f32)
    enc_share = lax.psum_scatter(
        grad_enc.astype(bf16), "dp", scatter_dimension=0, tiled=True
    )
    grad_bias = jnp.sum(lax.optimization_barrier(grad_pre).astype(f32), axis=0)
    bias_share = lax.psum_scatter(grad_bias, "dp", scatter_dimension=0, tiled=True)
    return (recon, enc_share[None], bias_share[None], jnp.stack(dec_parts), grad_b_dec)


def solution(mesh):
    placed = (
        P(("expert", "dp"), None),
        P(("expert", "dp")),
        P(("expert", "dp")),
        P(("expert", "dp")),
        P("expert", None, "layer"),
        P("expert", "layer"),
        P(None, "expert", "layer", None),
        P(None, "layer"),
        P(None, ("expert", "dp"), "layer"),
    )
    return jax.shard_map(
        local,
        mesh=mesh,
        in_specs=placed,
        out_specs=(
            P(None, ("expert", "dp"), "layer"),
            P("expert", "dp", "layer"),
            P("expert", ("layer", "dp")),
            P(None, "expert", "layer", "dp"),
            P(None, "layer"),
        ),
        check_vma=False,
    )
```

```python
import math

import jax
import jax.numpy as jnp
from jax import lax
from jax.sharding import PartitionSpec as P


def swap(values, mask):
    size = lax.axis_size("layer")
    return lax.ppermute(values, "layer", [(i, i ^ mask) for i in range(size)])


def gather_layers(piece, beside=None):
    size = lax.axis_size("layer")
    if size != 4 or piece.shape[0] % 2:
        return lax.all_gather(piece, "layer", axis=0, tiled=True), beside
    me = lax.axis_index("layer")
    depth = piece.shape[0]
    half = depth // 2
    near = swap(piece, 1)
    far = swap(piece, 2)
    if beside is not None:
        near, far, beside = lax.optimization_barrier((near, far, beside))
    first = swap(far[:half], 1)
    second = swap(near[half:], 2)
    whole = jnp.zeros((size * depth,) + piece.shape[1:], piece.dtype)
    for offset, value in (
        (me * depth, piece),
        ((me ^ 1) * depth, near),
        ((me ^ 2) * depth, far),
        ((me ^ 3) * depth, first),
        ((me ^ 3) * depth + half, second),
    ):
        whole = lax.dynamic_update_slice_in_dim(whole, value, offset, 0)
    return whole, beside


def scatter_sum(values):
    size = lax.axis_size("layer")
    depth = values.shape[0] // size
    if size != 4 or depth % 2:
        return lax.psum_scatter(values, "layer", scatter_dimension=0, tiled=True)
    f32 = jnp.float32
    me = lax.axis_index("layer")
    low, high = me % 2, me // 2
    pieces = values.reshape((2, 2, 2, depth // 2) + values.shape[1:])

    def pick(array, index, axis):
        return lax.dynamic_index_in_dim(array, index, axis, keepdims=False)

    one, two = pieces[:, :, 0], pieces[:, :, 1]
    one_in = swap(pick(one, 1 - low, 1), 1)
    two_in = swap(pick(two, 1 - high, 0), 2)
    one_sum = pick(one, low, 1).astype(f32) + one_in.astype(f32)
    two_sum = pick(two, high, 0).astype(f32) + two_in.astype(f32)
    one_last = swap(pick(one_sum, 1 - high, 0).astype(values.dtype), 2)
    two_last = swap(pick(two_sum, 1 - low, 0).astype(values.dtype), 1)
    return jnp.concatenate(
        [
            (pick(one_sum, high, 0) + one_last.astype(f32)).astype(values.dtype),
            (pick(two_sum, low, 0) + two_last.astype(f32)).astype(values.dtype),
        ]
    )


def local(tokens, expert_ids, slot_ids, live_mask, w_enc, b_enc, w_dec, b_dec, targets):
    f32, bf16 = jnp.float32, jnp.bfloat16
    n_expert = lax.axis_size("expert")
    n_layer = lax.axis_size("layer")
    n_dp = lax.axis_size("dp")
    tok_rows, model_width = tokens.shape
    capacity = 2 * tok_rows // n_expert
    total_cells = n_expert * capacity
    cell_index = expert_ids * capacity + slot_ids
    quarter = model_width // n_layer
    targets_count = w_dec.shape[0]
    enc_weight = w_enc[0]
    place = (
        lax.broadcasted_iota(jnp.int32, (total_cells, tok_rows), 0) == cell_index[None, :]
    ).astype(bf16)

    cells = lax.dot_general(
        tokens, place, (((0,), (1,)), ((), ())), preferred_element_type=f32
    ).astype(bf16)
    own = lax.dynamic_slice_in_dim(cells, lax.axis_index("layer") * quarter, quarter, 0)
    arrived_part = lax.all_to_all(own, "expert", split_axis=1, concat_axis=1, tiled=True)
    arrived, _ = gather_layers(arrived_part)
    pre_act = jnp.einsum("dr,dl->rl", arrived, enc_weight, preferred_element_type=f32)
    pre_act = pre_act + b_enc[0][None, :]
    active = jnp.maximum(pre_act, 0.0)
    latents = (active * active).astype(bf16)

    coef = 2.0 / math.sqrt(tok_rows)
    live_wide = live_mask.astype(f32)
    partials = [
        jnp.einsum("ld,rl->dr", w_dec[t, 0], latents, preferred_element_type=f32).astype(bf16)
        for t in range(targets_count)
    ]
    summed = [scatter_sum(p) for p in partials]
    recons, errors, parts = [], [], []
    for t in range(targets_count):
        returned = lax.all_to_all(summed[t], "expert", split_axis=1, concat_axis=1, tiled=True)
        recon_sum = jnp.einsum("dr,ri->di", returned, place, preferred_element_type=f32)
        recon_full = recon_sum + b_dec[t][:, None]
        recons.append(recon_full.astype(bf16).T)
        error = (
            coef * live_wide[None, :] * (recon_full - targets[t].T.astype(f32))
        ).astype(bf16)
        errors.append(jnp.sum(error.astype(f32), axis=1))
        outgoing = jnp.einsum(
            "di,ri->dr", error, place, preferred_element_type=f32
        ).astype(bf16)
        parts.append(
            lax.all_to_all(outgoing, "expert", split_axis=1, concat_axis=1, tiled=True)
        )
    recon = jnp.stack(recons)
    error_sums = lax.all_gather(jnp.stack(errors), ("expert", "dp"), axis=0)
    beside = parts[1:] + [error_sums]
    segments = []
    for t in range(targets_count):
        segment, beside[t] = gather_layers(parts[t], beside[t])
        if t + 1 < targets_count:
            parts[t + 1] = beside[t]
        else:
            error_sums = beside[t]
        segments.append(segment)
    grad_b_dec = jnp.sum(error_sums, axis=0)

    grad_lat = sum(
        jnp.einsum("dr,ld->rl", segments[t], w_dec[t, 0], preferred_element_type=f32)
        for t in range(targets_count)
    )
    halves = [
        jnp.einsum(
            "rl,hdr->hld",
            latents,
            segments[t].reshape(n_dp, model_width // n_dp, total_cells),
            preferred_element_type=f32,
        ).astype(bf16)
        for t in range(targets_count)
    ]
    dec_parts = [
        lax.psum_scatter(h, "dp", scatter_dimension=0, tiled=True) for h in halves
    ]
    grad_pre = (grad_lat * (2.0 * active)).astype(bf16)
    grad_enc = jnp.einsum("dr,rl->dl", arrived, grad_pre, preferred_element_type=f32)
    enc_share = lax.psum_scatter(
        grad_enc.astype(bf16), "dp", scatter_dimension=0, tiled=True
    )
    grad_bias = jnp.sum(lax.optimization_barrier(grad_pre).astype(f32), axis=0)
    bias_len = grad_bias.shape[0] // n_dp
    bias_share = lax.dynamic_slice_in_dim(
        lax.psum(grad_bias, "dp"), lax.axis_index("dp") * bias_len, bias_len, 0
    )
    return (recon, enc_share[None], bias_share[None], jnp.stack(dec_parts), grad_b_dec)


def solution(mesh):
    placed = (
        P(("expert", "dp"), None),
        P(("expert", "dp")),
        P(("expert", "dp")),
        P(("expert", "dp")),
        P("expert", None, "layer"),
        P("expert", "layer"),
        P(None, "expert", "layer", None),
        P(None, "layer"),
        P(None, ("expert", "dp"), "layer"),
    )
    return jax.shard_map(
        local,
        mesh=mesh,
        in_specs=placed,
        out_specs=(
            P(None, ("expert", "dp"), "layer"),
            P("expert", "dp", "layer"),
            P("expert", ("layer", "dp")),
            P(None, "expert", "layer", "dp"),
            P(None, "layer"),
        ),
        check_vma=False,
    )
```

```python
import math

import jax
import jax.numpy as jnp
from jax import lax
from jax.sharding import PartitionSpec as P


def swap(values, mask, axis="layer"):
    size = lax.axis_size(axis)
    return lax.ppermute(values, axis, [(i, i ^ mask) for i in range(size)])


def sum_all(values, axes):
    for axis in axes:
        size = lax.axis_size(axis)
        if size & (size - 1):
            values = lax.psum(values, axis)
            continue
        mask = 1
        while mask < size:
            values = values + swap(values, mask, axis)
            mask *= 2
    return values


def share_sum(product, rows, fills):
    depth = rows.shape[0] // 2
    me = lax.axis_index("dp")
    sent = product(lax.dynamic_slice_in_dim(rows, (1 - me) * depth, depth, 0))
    came = swap(sent.astype(fills), 1, "dp")
    own = product(lax.dynamic_slice_in_dim(rows, me * depth, depth, 0))
    return own + came.astype(jnp.float32)


def gather_layers(piece, beside=None):
    size = lax.axis_size("layer")
    if size != 4 or piece.shape[0] % 2:
        return lax.all_gather(piece, "layer", axis=0, tiled=True), beside
    me = lax.axis_index("layer")
    depth = piece.shape[0]
    half = depth // 2
    near = swap(piece, 1)
    far = swap(piece, 2)
    if beside is not None:
        near, far, beside = lax.optimization_barrier((near, far, beside))
    first = swap(far[:half], 1)
    second = swap(near[half:], 2)
    whole = jnp.zeros((size * depth,) + piece.shape[1:], piece.dtype)
    for offset, value in (
        (me * depth, piece),
        ((me ^ 1) * depth, near),
        ((me ^ 2) * depth, far),
        ((me ^ 3) * depth, first),
        ((me ^ 3) * depth + half, second),
    ):
        whole = lax.dynamic_update_slice_in_dim(whole, value, offset, 0)
    return whole, beside


def scatter_sum(values):
    size = lax.axis_size("layer")
    depth = values.shape[0] // size
    if size != 4 or depth % 2:
        return lax.psum_scatter(values, "layer", scatter_dimension=0, tiled=True)
    f32 = jnp.float32
    me = lax.axis_index("layer")
    low, high = me % 2, me // 2
    pieces = values.reshape((2, 2, 2, depth // 2) + values.shape[1:])

    def pick(array, index, axis):
        return lax.dynamic_index_in_dim(array, index, axis, keepdims=False)

    one, two = pieces[:, :, 0], pieces[:, :, 1]
    one_in = swap(pick(one, 1 - low, 1), 1)
    two_in = swap(pick(two, 1 - high, 0), 2)
    one_sum = pick(one, low, 1).astype(f32) + one_in.astype(f32)
    two_sum = pick(two, high, 0).astype(f32) + two_in.astype(f32)
    one_last = swap(pick(one_sum, 1 - high, 0).astype(values.dtype), 2)
    two_last = swap(pick(two_sum, 1 - low, 0).astype(values.dtype), 1)
    return jnp.concatenate(
        [
            (pick(one_sum, high, 0) + one_last.astype(f32)).astype(values.dtype),
            (pick(two_sum, low, 0) + two_last.astype(f32)).astype(values.dtype),
        ]
    )


def local(tokens, expert_ids, slot_ids, live_mask, w_enc, b_enc, w_dec, b_dec, targets):
    f32, bf16 = jnp.float32, jnp.bfloat16
    n_expert = lax.axis_size("expert")
    n_layer = lax.axis_size("layer")
    assert lax.axis_size("dp") == 2
    tok_rows, model_width = tokens.shape
    capacity = 2 * tok_rows // n_expert
    total_cells = n_expert * capacity
    cell_index = expert_ids * capacity + slot_ids
    quarter = model_width // n_layer
    targets_count = w_dec.shape[0]
    enc_weight = w_enc[0]
    place = (
        lax.broadcasted_iota(jnp.int32, (total_cells, tok_rows), 0) == cell_index[None, :]
    ).astype(bf16)

    cells = lax.dot_general(
        tokens, place, (((0,), (1,)), ((), ())), preferred_element_type=f32
    ).astype(bf16)
    own = lax.dynamic_slice_in_dim(cells, lax.axis_index("layer") * quarter, quarter, 0)
    arrived_part = lax.all_to_all(own, "expert", split_axis=1, concat_axis=1, tiled=True)
    arrived, _ = gather_layers(arrived_part)
    pre_act = jnp.einsum("dr,dl->rl", arrived, enc_weight, preferred_element_type=f32)
    pre_act = pre_act + b_enc[0][None, :]
    active = jnp.maximum(pre_act, 0.0)
    latents = (active * active).astype(bf16)

    coef = 2.0 / math.sqrt(tok_rows)
    live_wide = live_mask.astype(f32)
    partials = [
        jnp.einsum("ld,rl->dr", w_dec[t, 0], latents, preferred_element_type=f32).astype(bf16)
        for t in range(targets_count)
    ]
    summed = [scatter_sum(p) for p in partials]
    recons, errors, parts = [], [], []
    for t in range(targets_count):
        returned = lax.all_to_all(summed[t], "expert", split_axis=1, concat_axis=1, tiled=True)
        recon_sum = jnp.einsum("dr,ri->di", returned, place, preferred_element_type=f32)
        recon_full = recon_sum + b_dec[t][:, None]
        recons.append(recon_full.astype(bf16).T)
        error = (
            coef * live_wide[None, :] * (recon_full - targets[t].T.astype(f32))
        ).astype(bf16)
        errors.append(jnp.sum(error.astype(f32), axis=1))
        outgoing = jnp.einsum(
            "di,ri->dr", error, place, preferred_element_type=f32
        ).astype(bf16)
        parts.append(
            lax.all_to_all(outgoing, "expert", split_axis=1, concat_axis=1, tiled=True)
        )
    recon = jnp.stack(recons)
    grad_b_dec = sum_all(jnp.stack(errors), ("dp", "expert"))
    beside = parts[1:] + [None]
    segments = []
    for t in range(targets_count):
        segment, beside[t] = gather_layers(parts[t], beside[t])
        if t + 1 < targets_count:
            parts[t + 1] = beside[t]
        segments.append(segment)

    grad_lat = sum(
        jnp.einsum("dr,ld->rl", segments[t], w_dec[t, 0], preferred_element_type=f32)
        for t in range(targets_count)
    )
    dec_parts = [
        share_sum(
            lambda rows: jnp.einsum("dr,rl->dl", rows, latents, preferred_element_type=f32),
            segments[t],
            bf16,
        ).astype(bf16)
        for t in range(targets_count)
    ]
    grad_pre = (grad_lat * (2.0 * active)).astype(bf16)
    enc_share = share_sum(
        lambda rows: jnp.einsum("dr,rl->dl", rows, grad_pre, preferred_element_type=f32),
        arrived,
        bf16,
    ).astype(bf16)
    grad_bias = jnp.sum(lax.optimization_barrier(grad_pre).astype(f32), axis=0)
    bias_share = share_sum(lambda rows: rows, grad_bias, f32)
    dec_share = jnp.stack([part.T for part in dec_parts])[:, None]
    return (recon, enc_share[None], bias_share[None], dec_share, grad_b_dec)


def solution(mesh):
    placed = (
        P(("expert", "dp"), None),
        P(("expert", "dp")),
        P(("expert", "dp")),
        P(("expert", "dp")),
        P("expert", None, "layer"),
        P("expert", "layer"),
        P(None, "expert", "layer", None),
        P(None, "layer"),
        P(None, ("expert", "dp"), "layer"),
    )
    return jax.shard_map(
        local,
        mesh=mesh,
        in_specs=placed,
        out_specs=(
            P(None, ("expert", "dp"), "layer"),
            P("expert", "dp", "layer"),
            P("expert", ("layer", "dp")),
            P(None, "expert", "layer", "dp"),
            P(None, "layer"),
        ),
        check_vma=False,
    )
```

```python
import math

import jax
import jax.numpy as jnp
from jax import lax
from jax.sharding import PartitionSpec as P


def swap(values, mask, axis="layer"):
    size = lax.axis_size(axis)
    return lax.ppermute(values, axis, [(i, i ^ mask) for i in range(size)])


def exchange_experts(values):
    size = lax.axis_size("expert")
    if size != 4:
        return lax.all_to_all(values, "expert", split_axis=1, concat_axis=1, tiled=True)
    width = values.shape[1] // size
    blocks = [values[:, k * width : (k + 1) * width] for k in range(size)]
    for mask in (2, 3, 1):
        blocks[mask] = swap(blocks[mask], mask, "expert")
    return jnp.concatenate(blocks, axis=1)


def sum_all(values, axes):
    for axis in axes:
        size = lax.axis_size(axis)
        if size & (size - 1):
            values = lax.psum(values, axis)
            continue
        mask = 1
        while mask < size:
            values = values + swap(values, mask, axis)
            mask *= 2
    return values


def share_sum(product, rows, fills):
    depth = rows.shape[0] // 2
    me = lax.axis_index("dp")
    sent = product(lax.dynamic_slice_in_dim(rows, (1 - me) * depth, depth, 0))
    came = swap(sent.astype(fills), 1, "dp")
    own = product(lax.dynamic_slice_in_dim(rows, me * depth, depth, 0))
    return own + came.astype(jnp.float32)


def gather_layers(piece, beside=None):
    size = lax.axis_size("layer")
    if size != 4 or piece.shape[0] % 2:
        return lax.all_gather(piece, "layer", axis=0, tiled=True), beside
    me = lax.axis_index("layer")
    depth = piece.shape[0]
    half = depth // 2
    near = swap(piece, 1)
    far = swap(piece, 2)
    if beside is not None:
        near, far, beside = lax.optimization_barrier((near, far, beside))
    first = swap(far[:half], 1)
    second = swap(near[half:], 2)
    whole = jnp.zeros((size * depth,) + piece.shape[1:], piece.dtype)
    for offset, value in (
        (me * depth, piece),
        ((me ^ 1) * depth, near),
        ((me ^ 2) * depth, far),
        ((me ^ 3) * depth, first),
        ((me ^ 3) * depth + half, second),
    ):
        whole = lax.dynamic_update_slice_in_dim(whole, value, offset, 0)
    return whole, beside


def scatter_sum(values):
    size = lax.axis_size("layer")
    depth = values.shape[0] // size
    if size != 4 or depth % 2:
        return lax.psum_scatter(values, "layer", scatter_dimension=0, tiled=True)
    f32 = jnp.float32
    me = lax.axis_index("layer")
    low, high = me % 2, me // 2
    pieces = values.reshape((2, 2, 2, depth // 2) + values.shape[1:])

    def pick(array, index, axis):
        return lax.dynamic_index_in_dim(array, index, axis, keepdims=False)

    one, two = pieces[:, :, 0], pieces[:, :, 1]
    one_in = swap(pick(one, 1 - low, 1), 1)
    two_in = swap(pick(two, 1 - high, 0), 2)
    one_sum = pick(one, low, 1).astype(f32) + one_in.astype(f32)
    two_sum = pick(two, high, 0).astype(f32) + two_in.astype(f32)
    one_last = swap(pick(one_sum, 1 - high, 0).astype(values.dtype), 2)
    two_last = swap(pick(two_sum, 1 - low, 0).astype(values.dtype), 1)
    return jnp.concatenate(
        [
            (pick(one_sum, high, 0) + one_last.astype(f32)).astype(values.dtype),
            (pick(two_sum, low, 0) + two_last.astype(f32)).astype(values.dtype),
        ]
    )


def local(tokens, expert_ids, slot_ids, live_mask, w_enc, b_enc, w_dec, b_dec, targets):
    f32, bf16 = jnp.float32, jnp.bfloat16
    n_expert = lax.axis_size("expert")
    n_layer = lax.axis_size("layer")
    assert lax.axis_size("dp") == 2
    tok_rows, model_width = tokens.shape
    capacity = 2 * tok_rows // n_expert
    total_cells = n_expert * capacity
    offset = lax.axis_index("expert") if n_expert == 4 else 0
    cell_index = (expert_ids ^ offset) * capacity + slot_ids
    quarter = model_width // n_layer
    targets_count = w_dec.shape[0]
    enc_weight = w_enc[0]
    place = (
        lax.broadcasted_iota(jnp.int32, (total_cells, tok_rows), 0) == cell_index[None, :]
    ).astype(bf16)

    cells = lax.dot_general(
        tokens, place, (((0,), (1,)), ((), ())), preferred_element_type=f32
    ).astype(bf16)
    own = lax.dynamic_slice_in_dim(cells, lax.axis_index("layer") * quarter, quarter, 0)
    arrived_part = exchange_experts(own)
    arrived, _ = gather_layers(arrived_part)
    pre_act = jnp.einsum("dr,dl->rl", arrived, enc_weight, preferred_element_type=f32)
    pre_act = pre_act + b_enc[0][None, :]
    active = jnp.maximum(pre_act, 0.0)
    latents = (active * active).astype(bf16)

    coef = 2.0 / math.sqrt(tok_rows)
    live_wide = live_mask.astype(f32)
    partials = [
        jnp.einsum("ld,rl->dr", w_dec[t, 0], latents, preferred_element_type=f32).astype(bf16)
        for t in range(targets_count)
    ]
    summed = [scatter_sum(p) for p in partials]
    recons, errors, parts = [], [], []
    for t in range(targets_count):
        returned = exchange_experts(summed[t])
        recon_sum = jnp.einsum("dr,ri->di", returned, place, preferred_element_type=f32)
        recon_full = recon_sum + b_dec[t][:, None]
        recons.append(recon_full.astype(bf16).T)
        error = (
            coef * live_wide[None, :] * (recon_full - targets[t].T.astype(f32))
        ).astype(bf16)
        errors.append(jnp.sum(error.astype(f32), axis=1))
        outgoing = jnp.einsum(
            "di,ri->dr", error, place, preferred_element_type=f32
        ).astype(bf16)
        parts.append(exchange_experts(outgoing))
    recon = jnp.stack(recons)
    grad_b_dec = sum_all(jnp.stack(errors), ("dp", "expert"))
    beside = parts[1:] + [None]
    segments = []
    for t in range(targets_count):
        segment, beside[t] = gather_layers(parts[t], beside[t])
        if t + 1 < targets_count:
            parts[t + 1] = beside[t]
        segments.append(segment)

    grad_lat = sum(
        jnp.einsum("dr,ld->rl", segments[t], w_dec[t, 0], preferred_element_type=f32)
        for t in range(targets_count)
    )
    dec_parts = [
        share_sum(
            lambda rows: jnp.einsum("dr,rl->dl", rows, latents, preferred_element_type=f32),
            segments[t],
            bf16,
        ).astype(bf16)
        for t in range(targets_count)
    ]
    grad_pre = (grad_lat * (2.0 * active)).astype(bf16)
    enc_share = share_sum(
        lambda rows: jnp.einsum("dr,rl->dl", rows, grad_pre, preferred_element_type=f32),
        arrived,
        bf16,
    ).astype(bf16)
    grad_bias = jnp.sum(lax.optimization_barrier(grad_pre).astype(f32), axis=0)
    bias_share = share_sum(lambda rows: rows, grad_bias, f32)
    dec_share = jnp.stack([part.T for part in dec_parts])[:, None]
    return (recon, enc_share[None], bias_share[None], dec_share, grad_b_dec)


def solution(mesh):
    placed = (
        P(("expert", "dp"), None),
        P(("expert", "dp")),
        P(("expert", "dp")),
        P(("expert", "dp")),
        P("expert", None, "layer"),
        P("expert", "layer"),
        P(None, "expert", "layer", None),
        P(None, "layer"),
        P(None, ("expert", "dp"), "layer"),
    )
    return jax.shard_map(
        local,
        mesh=mesh,
        in_specs=placed,
        out_specs=(
            P(None, ("expert", "dp"), "layer"),
            P("expert", "dp", "layer"),
            P("expert", ("layer", "dp")),
            P(None, "expert", "layer", "dp"),
            P(None, "layer"),
        ),
        check_vma=False,
    )
```
